256 devices in a mesh: grp: 8 (over y, x_hi), tok: 32 (over z, x_lo, core).
Axes of the slice: x: 4 (x_hi: 2, x_lo: 2; x = x_hi * 2 + x_lo), y: 4, z: 8, core: 2. Of those that a mesh axis runs over, the one named last changes fastest.
Arguments:
- layer_input: bfloat16 [8, 6144, 1536], P('grp', 'tok'), may hold values from -54 to 54
- attn_gain: float32 [1536], replicated, may hold values from 0.1 to 1.9
- w_query: bfloat16 [1536, 1536], P('tok'), may hold values from -0.15625 to 0.15625
- w_keyval: bfloat16 [1536, 1024], P('tok'), may hold values from -0.15625 to 0.15625
- w_output: bfloat16 [1536, 1536], P('tok'), may hold values from -0.15625 to 0.15625
- prefix_cache: bfloat16 [8, 512, 1024], P('grp', 'tok'), may hold values from -260 to 260
- lengths: int32 [8, 48], P('grp'), may hold values from 1 to 192, 6144 in all within a row
- moe_gain: float32 [1536], replicated, may hold values from 0.1 to 1.9
- w_router: bfloat16 [1536, 16], replicated, may hold values from -0.15625 to 0.15625
- routes: int32 [8, 6144, 2], P('grp', 'tok'), may hold values from 0 to 15, all different within a row; in each aligned block of 192 rows (0 to 191, 192 to 383, ..., all dimensions but the last counted through in order) at most 30 rows name the same one
- w_expert_in: bfloat16 [32, 1536, 1024], P('tok', 'grp'), may hold values from -0.15625 to 0.15625
- w_expert_out: bfloat16 [32, 512, 1536], P('tok', 'grp'), may hold values from -0.1875 to 0.1875
Outputs:
- hidden: bfloat16 [8, 6144, 1536], P('grp', 'tok')
- suffix_cache: bfloat16 [8, 6144, 1024], P('grp', 'tok')
The draws below stay inside these ranges and needn't reach their ends.
Inputs may be any that keep to these rules, and one draw needn't show every extreme that they name: `lengths`: each row sums to 6144, and its largest length is 192. A token's 2 routes differ. Among the rows of one device no expert is named more than 30 times, a bound that some block reaches in some devices' rows.
All inputs are finite; a program needn't handle non-finite values.
Results may differ from the reference program's by a relative error of at most 0.0073.
The reference program's roundings to bfloat16 on the way (of `normed`, `attended`, `normed2`, `act` and `expert_out`) count: a program that leaves them out, or rounds other values in their place, can miss the bound.
Values may be sent and summed in bfloat16 or wider, within the bound.
A program may use at most 64 MiB of HBM per device.

```python
import math
import jax
import jax.numpy as jnp
import numpy as np
from jax import lax

D = 1536
HEADS = 24
KV_HEADS = 8
HEAD_DIM = 64
FF = 1024
TOP = 2
TOK_DEV = 192
GROUPS = 8
SUFFIX = 6144
PREFIX = 512
REQS = 48
EXPERTS = 16
CAP = 30
N_TOK = 32


def draw_layer_input(key, part):
    keys = jax.random.split(key, 3)
    row_scale = jnp.exp(jax.random.uniform(keys[0], (GROUPS, SUFFIX, 1), jnp.float32, math.log(0.3), math.log(3.0)))
    col_scale = jnp.exp(jax.random.uniform(keys[1], (1, 1, D), jnp.float32, math.log(0.3), math.log(3.0)))
    noise = jnp.clip(jax.random.normal(keys[2], (GROUPS, SUFFIX, D), jnp.float32), -6.0, 6.0)
    return (noise * row_scale * col_scale).astype(jnp.bfloat16)


def draw_prefix_cache(key, part):
    keys = jax.random.split(key, 1)
    kv_width = KV_HEADS * HEAD_DIM
    base = jnp.clip(jax.random.normal(keys[0], (GROUPS, PREFIX, 2 * kv_width), jnp.float32), -6.0, 6.0)
    return base.astype(jnp.bfloat16)


def shard_levels(own_key, extent, pieces, least, high):
    gain = 1.0
    for axis_at, blocks in pieces:
        heights = jax.random.uniform(jax.random.fold_in(jax.random.fold_in(own_key, 6), axis_at), (blocks,), jnp.float32, least / len(pieces), high / len(pieces))
        gain = gain * jnp.repeat(jnp.exp(heights), extent[axis_at] // blocks).reshape((-1,) + (1,) * (len(extent) - 1 - axis_at))
    return gain


def split_up(number_of, total, limit, lean):
    portions = [(1 << 20) // math.isqrt(rank ** lean) + 1 for rank in range(2, number_of + 1)]
    surplus, given = total - limit - (number_of - 1), [1] * (number_of - 1)
    while surplus > 0:
        free = [i for i in range(number_of - 1) if given[i] < limit]
        whole, left = sum([portions[i] for i in free]), surplus
        for i in free:
            addition = min(limit - given[i], max(1, left * portions[i] // whole), surplus)
            given[i] = given[i] + addition
            surplus = surplus - addition
    return np.array([limit] + given)


def uneven_parts(key, amount, total, most, skew):
    if amount == 2:
        one = jax.random.randint(key, (), max(1, total - most), min(most, total - 1) + 1)
        return jnp.stack([one, total - one])
    sizes = jnp.asarray(split_up(amount, total, most, skew), jnp.int32)
    couples = (amount - 1) // 2
    source_of, sink = sizes[1:1 + 2 * couples:2], sizes[2:2 + 2 * couples:2]
    margin = jnp.minimum(source_of - 1, most - sink)
    shifted = jax.random.randint(jax.random.fold_in(key, 1), (couples,), 0, 1 << 20) % (margin + 1)
    sizes = sizes.at[1:1 + 2 * couples:2].set(source_of - shifted).at[2:2 + 2 * couples:2].set(sink + shifted)
    return sizes[jax.random.permutation(jax.random.fold_in(key, 2), amount)]


def routed_block(stream_key, own, number, rows, number_of, top, bound, lean):
    order = jax.random.permutation(stream_key, number_of)
    heavy_load, usual = portions_of(number_of, rows * top, bound, lean, True), portions_of(number_of, rows * top, bound, lean, False)
    places = jnp.arange(number_of)

    def named(tallies, rotation):
        used = int((tallies > 0).sum())
        fixed = max(1, used // 4)
        shifted = fixed + (places - fixed + rotation * (used - fixed)) % max(1, number_of - fixed)
        return jnp.zeros((number_of,), jnp.int32).at[order[jnp.where(places < fixed, places, shifted)]].set(jnp.asarray(tallies, jnp.int32))

    tallies = jnp.where(number % 4 == 0, named(heavy_load, number // 4), named(usual, number - number // 4 - 1))
    mixed = jax.random.permutation(jax.random.fold_in(own, 3), number_of)
    giver, receiver = mixed[0:number_of // 2 * 2:2], mixed[1:number_of // 2 * 2:2]
    slack = jnp.minimum(tallies[giver] - 1, bound - tallies[receiver]) // 2
    slack = jnp.where((giver == order[0]) | (receiver == order[0]) | (tallies[receiver] == 0), 0, jnp.maximum(slack, 0))
    shifted = jax.random.randint(jax.random.fold_in(own, 4), (number_of // 2,), 0, 1 << 20) % (slack + 1)
    tallies = tallies.at[giver].add(-shifted).at[receiver].add(shifted)
    members = jnp.searchsorted(jnp.cumsum(tallies), jnp.arange(rows * top), side="right").astype(jnp.int32)
    grid = members.reshape(top, rows).T
    grid = grid[jax.random.permutation(jax.random.fold_in(own, 1), rows)]
    rotation = jax.random.randint(jax.random.fold_in(own, 2), (rows, 1), 0, top)
    return jnp.take_along_axis(grid, (jnp.arange(top)[None, :] + rotation) % top, axis=1)


def portions_of(amount, total, reach, slope, full):
    portions = [(1 << 20) // math.isqrt(rank ** slope) + 1 for rank in range(1, amount + 1)]
    largest = reach if full else min(reach, max(-(-total // amount), total * portions[0] // sum(portions)))
    least = 1 if total - largest >= amount - 1 else 0
    counts, surplus = [largest] + [least] * (amount - 1), total - largest - least * (amount - 1)
    while surplus > 0:
        candidates = [i for i in range(1, amount) if counts[i] < largest] or [i for i in range(1, amount) if counts[i] < reach]
        mass, remaining = sum([portions[i] for i in candidates]), surplus
        for i in candidates:
            addition = min(reach - counts[i], max(1, remaining * portions[i] // mass), surplus)
            counts[i] = counts[i] + addition
            surplus = surplus - addition
    return np.array(counts)


def centred(rng, dims, spread, reach, cuts=(), held_as=jnp.bfloat16):
    level = shard_levels(rng, dims, cuts, -0.22, 0.18) if cuts else 1.0
    result = jax.random.normal(rng, dims, jnp.float32) * spread * level
    return jnp.minimum(jnp.maximum(result, -reach), reach).astype(held_as)


def setup_inputs(seed: int = 0) -> dict:
    arg_keys = jax.random.split(jax.random.key(seed), 13)
    layer_input = draw_layer_input(jax.random.fold_in(arg_keys[12], 71), 0)
    attn_gain = jnp.clip(1.0 + 0.18 * jax.random.normal(arg_keys[1], (D,), jnp.float32), 0.1, 1.9)
    w_query = centred(arg_keys[2], (D, HEADS * HEAD_DIM), D ** -0.5, 0.15625, ((0, 32),))
    w_keyval = centred(arg_keys[3], (D, 2 * KV_HEADS * HEAD_DIM), D ** -0.5, 0.15625, ((0, 32),))
    w_output = centred(arg_keys[4], (HEADS * HEAD_DIM, D), (HEADS * HEAD_DIM) ** -0.5, 0.15625, ((0, 32),))
    prefix_cache = draw_prefix_cache(jax.random.fold_in(arg_keys[12], 71), 0)
    lengths = jax.vmap(lambda own: uneven_parts(own, REQS, SUFFIX, TOK_DEV, 2))(jax.random.split(arg_keys[6], GROUPS)).reshape((GROUPS, REQS)).astype(jnp.int32)
    moe_gain = jnp.clip(1.0 + 0.18 * jax.random.normal(arg_keys[7], (D,), jnp.float32), 0.1, 1.9)
    w_router = centred(arg_keys[8], (D, EXPERTS), D ** -0.5, 0.15625)
    routes_keys = jax.random.split(jax.random.fold_in(arg_keys[9], 1), GROUPS * SUFFIX // TOK_DEV)
    routes_turns = jax.random.permutation(jax.random.fold_in(arg_keys[9], 3), GROUPS * SUFFIX // TOK_DEV)
    routes = jax.vmap(lambda own, number: routed_block(jax.random.fold_in(arg_keys[9], 2), own, number, TOK_DEV, EXPERTS, TOP, CAP, 1))(routes_keys, routes_turns).reshape((GROUPS, SUFFIX, TOP))
    w_expert_in = centred(arg_keys[10], (2 * EXPERTS, D, FF), D ** -0.5, 0.15625, ((0, 32), (1, 8)))
    w_expert_out = centred(arg_keys[11], (2 * EXPERTS, FF // 2, D), FF ** -0.5, 0.1875, ((0, 32), (1, 8)))
    return dict(layer_input=layer_input, attn_gain=attn_gain, w_query=w_query, w_keyval=w_keyval, w_output=w_output, prefix_cache=prefix_cache, lengths=lengths, moe_gain=moe_gain, w_router=w_router, routes=routes, w_expert_in=w_expert_in, w_expert_out=w_expert_out)


EPS = 1e-05

def rms_scale(inputs, scale_row):
    inputs = inputs.astype(jnp.float32)
    inverse = lax.rsqrt(lax.optimization_barrier(jnp.mean(inputs * inputs, axis=-1, keepdims=True)) + EPS)
    return inputs * inverse * scale_row

def segment_of(req_lengths, positions):
    request_ends = jnp.cumsum(req_lengths, dtype=jnp.int32)
    return lax.optimization_barrier(jnp.sum((request_ends[None, :] <= positions[:, None]).astype(jnp.int32), axis=1)).astype(jnp.int32)

def group_attention(queries, keyval, prefix, req_lengths):
    kv_width = KV_HEADS * HEAD_DIM
    group_share = HEADS // KV_HEADS
    blocks = SUFFIX // TOK_DEV
    padded = jnp.concatenate([jnp.zeros((TOK_DEV, 2 * kv_width), keyval.dtype), keyval], axis=0)
    positions = jnp.arange(SUFFIX, dtype=jnp.int32)
    segments = segment_of(req_lengths, positions)
    seg_padded = jnp.concatenate([-jnp.ones((TOK_DEV,), jnp.int32), segments])
    pre_keys = prefix[:, :kv_width].astype(jnp.float32).reshape(PREFIX, KV_HEADS, HEAD_DIM)
    pre_values = prefix[:, kv_width:].astype(jnp.float32).reshape(PREFIX, KV_HEADS, HEAD_DIM)

    def one_block(block_index):
        first_row = (block_index * TOK_DEV).astype(jnp.int32)
        q_rows = lax.dynamic_slice_in_dim(queries, first_row, TOK_DEV, 0).astype(jnp.float32)
        q_rows = q_rows.reshape(TOK_DEV, KV_HEADS, group_share, HEAD_DIM)
        near_block = lax.dynamic_slice_in_dim(padded, first_row, 2 * TOK_DEV, 0).astype(jnp.float32)
        near_seg = lax.dynamic_slice_in_dim(seg_padded, first_row, 2 * TOK_DEV, 0)
        q_seg = lax.dynamic_slice_in_dim(segments, first_row, TOK_DEV, 0)
        key_pos = first_row - TOK_DEV + jnp.arange(2 * TOK_DEV, dtype=jnp.int32)
        q_pos = first_row + jnp.arange(TOK_DEV, dtype=jnp.int32)
        allowed = (near_seg[None, :] == q_seg[:, None]) & (key_pos[None, :] <= q_pos[:, None])
        key_rows = jnp.concatenate([pre_keys, near_block[:, :kv_width].reshape(2 * TOK_DEV, KV_HEADS, HEAD_DIM)], axis=0)
        value_rows = jnp.concatenate([pre_values, near_block[:, kv_width:].reshape(2 * TOK_DEV, KV_HEADS, HEAD_DIM)], axis=0)
        mask = jnp.concatenate([jnp.ones((TOK_DEV, PREFIX), bool), allowed], axis=1)
        scores = jnp.einsum('tkgd,skd->tkgs', q_rows, key_rows) * HEAD_DIM ** (-0.5)
        scores = jnp.where(mask[:, None, None, :], scores, -jnp.inf)
        top_score = lax.optimization_barrier(jnp.max(scores, axis=-1, keepdims=True))
        weights = jnp.exp(scores - top_score)
        accumulated = lax.optimization_barrier(jnp.sum(weights, axis=-1))
        rounded = weights.astype(jnp.bfloat16).astype(jnp.float32)
        numerators = jnp.einsum('tkgs,skd->tkgd', rounded, value_rows)
        return (numerators / accumulated[..., None]).astype(jnp.bfloat16).reshape(TOK_DEV, HEADS * HEAD_DIM)
    return lax.map(one_block, jnp.arange(blocks, dtype=jnp.int32)).reshape(SUFFIX, HEADS * HEAD_DIM)

def group_experts(normed2, chosen, gate_weights, w_expert_in, w_expert_out):
    flat_routes = chosen.reshape(-1)
    flat_gates = gate_weights.reshape(-1)
    capacity_all = N_TOK * CAP
    half_units = FF // 2

    def one_expert(accumulated, expert):
        picked = jnp.nonzero(flat_routes == expert, size=capacity_all, fill_value=0)[0].astype(jnp.int32)
        count = jnp.sum((flat_routes == expert).astype(jnp.int32))
        valid = (jnp.arange(capacity_all, dtype=jnp.int32) < count).astype(jnp.float32)
        token_index = (picked // TOP).astype(jnp.int32)
        inputs = normed2[token_index]
        w_pair = lax.dynamic_slice_in_dim(w_expert_in, (2 * expert).astype(jnp.int32), 2, 0)
        gate_w = jnp.concatenate([w_pair[0][:, :half_units], w_pair[1][:, :half_units]], axis=1)
        up_w = jnp.concatenate([w_pair[0][:, half_units:], w_pair[1][:, half_units:]], axis=1)
        down_w = lax.dynamic_slice_in_dim(w_expert_out, (2 * expert).astype(jnp.int32), 2, 0).reshape(FF, D)
        gate_part = jnp.dot(inputs, gate_w, preferred_element_type=jnp.float32)
        up_part = jnp.dot(inputs, up_w, preferred_element_type=jnp.float32)
        act = (jax.nn.silu(gate_part) * up_part).astype(jnp.bfloat16)
        expert_out = jnp.dot(act, down_w, preferred_element_type=jnp.float32).astype(jnp.bfloat16)
        expert_out = lax.optimization_barrier(expert_out).astype(jnp.float32)
        scaled = expert_out * (flat_gates[picked] * valid)[:, None]
        return (accumulated.at[token_index].add(scaled), None)
    accumulated, unused = lax.scan(one_expert, jnp.zeros((SUFFIX, D), jnp.float32), jnp.arange(EXPERTS, dtype=jnp.int32))
    return accumulated

def reference(layer_input, attn_gain, w_query, w_keyval, w_output, prefix_cache, lengths, moe_gain, w_router, routes, w_expert_in, w_expert_out):

    def one_group(group_args):
        tokens, prefix, req_lengths, chosen = group_args
        normed = rms_scale(tokens, attn_gain).astype(jnp.bfloat16)
        queries = jnp.dot(normed, w_query, preferred_element_type=jnp.float32).astype(jnp.bfloat16)
        keyval = jnp.dot(normed, w_keyval, preferred_element_type=jnp.float32).astype(jnp.bfloat16)
        attended = group_attention(queries, keyval, prefix, req_lengths)
        residual = tokens.astype(jnp.float32) + jnp.dot(attended, w_output, preferred_element_type=jnp.float32)
        normed2 = rms_scale(residual, moe_gain).astype(jnp.bfloat16)
        logits = jnp.dot(normed2, w_router, preferred_element_type=jnp.float32)
        picked = jnp.take_along_axis(logits, chosen, axis=1)
        scores = jax.nn.sigmoid(picked)
        gate_weights = scores / lax.optimization_barrier(jnp.sum(scores, axis=-1, keepdims=True))
        moe_part = group_experts(normed2, chosen, gate_weights, w_expert_in, w_expert_out)
        return ((residual + moe_part).astype(jnp.bfloat16), keyval)
    hidden, suffix_cache = lax.map(one_group, (layer_input, prefix_cache, lengths, routes))
    return (hidden, suffix_cache)
```

```python
import jax
import jax.numpy as jnp
from jax import lax
from jax.experimental import pallas as pl
from jax.experimental.pallas import tpu as pltpu
from jax.sharding import PartitionSpec as P

MESH = pl.DeviceIdType.MESH
Z, Y, X = 8, 4, 4
SLOTS = 32
N_COPIES = 160

HEADS = 24
KV_HEADS = 8
HEAD_DIM = 64
TOP = 2


EPS = 1e-05


def passed_along(value, axis, steps):
    count = lax.axis_size(axis)
    initial, last = (max(0, -steps), min(count, count - steps))
    return lax.ppermute(value, axis, [(source, source + steps) for source in range(initial, last)])


def rms_scale(inputs, scale_row):
    inputs = inputs.astype(jnp.float32)
    inverse = lax.rsqrt(jnp.mean(inputs * inputs, axis=-1, keepdims=True) + EPS)
    return inputs * inverse * scale_row


def segment_of(req_lengths, positions):
    request_ends = jnp.cumsum(req_lengths, dtype=jnp.int32)
    return jnp.sum((request_ends[None, :] <= positions[:, None]).astype(jnp.int32), axis=1)


def product(left, right):
    return jnp.dot(left, right, preferred_element_type=jnp.float32)


def greet(devices):
    barrier = pltpu.get_barrier_semaphore()
    for device in devices:
        pl.semaphore_signal(barrier, inc=1, device_id=device, device_id_type=MESH)
    pl.semaphore_wait(barrier, len(devices))


def gather_kernel(
    qkv, wo, pre, win, wout,
    qkv_all, wo_all, pre_all, win_own, win_other, wout_own, wout_other,
    relay_in, relay_out, send, recv, local,
):
    g, t = lax.axis_index("grp"), lax.axis_index("tok")
    y, xh = g // 2, g % 2
    z, xl, core = t // 4, (t // 2) % 2, t % 2
    x = xh * 2 + xl

    def at_x(step):
        nx = (x + step + X) % X
        return (y * 2 + nx // 2, z * 4 + (nx % 2) * 2 + core)

    def at_z(step):
        return (g, ((z + step + Z) % Z) * 4 + xl * 2 + core)

    def at_y(step):
        return (((y + step + Y) % Y) * 2 + xh, t)

    x_up, x_down = at_x(1), at_x(-1)
    z_up, z_down, y_up, y_down = at_z(1), at_z(-1), at_y(1), at_y(-1)
    mate = (g, z * 4 + xl * 2 + 1 - core)
    pair = (g, z * 4 + (1 - xl) * 2 + core)

    def tok_at(dz, parity, other_core=0):
        lane = (1 - xl) if parity else xl
        side = (1 - core) if other_core else core
        return ((z + dz + Z) % Z) * 4 + lane * 2 + side

    def grp_at(dy, across):
        return ((y + dy + Y) % Y) * 2 + ((1 - xh) if across else xh)

    slots, sends = {}, []

    def start(name, src, dst, device):
        slots[name] = len(slots)
        copy = pltpu.make_async_remote_copy(
            src_ref=src, dst_ref=dst, send_sem=send.at[slots[name]],
            recv_sem=recv.at[slots[name]], device_id=device, device_id_type=MESH,
        )
        copy.start()
        sends.append(copy)

    def arrived(name, dst):
        pltpu.make_async_remote_copy(
            src_ref=dst, dst_ref=dst, send_sem=send.at[slots[name]],
            recv_sem=recv.at[slots[name]], device_id=mate, device_id_type=MESH,
        ).wait_recv()

    greet([x_up, x_down, z_up, z_down, y_up, y_down, mate])

    own = []
    for src, dst in (
        (qkv, qkv_all.at[t]), (wo, wo_all.at[t]), (pre, pre_all.at[t]),
        (win, win_own.at[g]), (wout, wout_own.at[g]),
    ):
        own.append(pltpu.make_async_copy(src, dst, local.at[len(own)]))
        own[-1].start()

    def along_z(k, src_up, src_down):
        up, down = tok_at(1 - k, 0), tok_at(k - 1, 0)
        start(("up", "pre", k), src_up[2], pre_all.at[up], z_up)
        start(("up", "qkv", k), src_up[0], qkv_all.at[up], z_up)
        if k < 4:
            start(("up", "wo", k), src_up[1], wo_all.at[up], z_up)
            start(("down", "pre", k), src_down[2], pre_all.at[down], z_down)
            start(("down", "qkv", k), src_down[0], qkv_all.at[down], z_down)
        start(("down", "wo", k), src_down[1], wo_all.at[down], z_down)

    def to_mate(dz, parity, src):
        at = tok_at(dz, parity)
        start(("mate", "qkv", dz, parity), src[0], qkv_all.at[at], mate)
        start(("mate", "wo", dz, parity), src[1], wo_all.at[at], mate)
        start(("mate", "pre", dz, parity), src[2], pre_all.at[at], mate)

    def along_x(dz, src):
        at = tok_at(dz, 0)
        start(("x", "pre", dz), src[2], pre_all.at[at], pair)
        start(("x", "qkv", dz), src[0], qkv_all.at[at], x_up)
        start(("x", "wo", dz), src[1], wo_all.at[at], x_down)
        to_mate(dz, 0, src)

    def held(at):
        return (qkv_all.at[at], wo_all.at[at], pre_all.at[at])

    def from_x(dz):
        at = tok_at(dz, 1)
        for name, ref in (("pre", pre_all), ("qkv", qkv_all), ("wo", wo_all)):
            arrived(("x", name, dz), ref.at[at])
        to_mate(dz, 1, held(at))

    def expert_mate(dy, across, src):
        at = grp_at(dy, across)
        start(("mate", "win", dy, across), src[0], win_other.at[at], mate)
        start(("mate", "wout", dy, across), src[1], wout_other.at[at], mate)

    def along_y(across, src):
        at = grp_at(0, across)
        for way, device in (("yup", y_up), ("ydown", y_down)):
            start((way, "win", across), src[0], win_own.at[at], device)
            start((way, "wout", across), src[1], wout_own.at[at], device)
        expert_mate(0, across, src)

    def expert_held(at):
        return (win_own.at[at], wout_own.at[at])

    part = 144

    def from_y(across):
        at = grp_at(-1, across)
        arrived(("yup", "win", across), win_own.at[at])
        start(("yup2", "win", across), win_own.at[at, pl.ds(0, part)],
              win_own.at[at, pl.ds(0, part)], y_up)
        arrived(("yup", "wout", across), wout_own.at[at])
        expert_mate(-1, across, expert_held(at))
        at = grp_at(1, across)
        rest = 192 - part
        arrived(("ydown", "win", across), win_own.at[at])
        start(("ydown2", "win", across), win_own.at[at, pl.ds(part, rest)],
              win_own.at[at, pl.ds(part, rest)], y_down)
        arrived(("ydown", "wout", across), wout_own.at[at])
        start(("ydown2", "wout", across), wout_own.at[at], wout_own.at[at], y_down)
        expert_mate(1, across, expert_held(at))

    def from_y_far(across):
        at = grp_at(2, across)
        arrived(("yup2", "win", across), win_own.at[at, pl.ds(0, part)])
        arrived(("ydown2", "win", across), win_own.at[at, pl.ds(part, 192 - part)])
        arrived(("ydown2", "wout", across), wout_own.at[at])
        expert_mate(2, across, expert_held(at))

    mine = (qkv, wo, pre)
    along_z(1, mine, mine)
    start(("relay", "win"), win, relay_in, x_down)
    start(("relay", "wout"), wout, relay_out, x_down)
    along_y(0, (win, wout))
    along_x(0, mine)

    for k in (1, 2, 3):
        for name, ref in (("pre", pre_all), ("qkv", qkv_all), ("wo", wo_all)):
            arrived(("up", name, k), ref.at[tok_at(-k, 0)])
            arrived(("down", name, k), ref.at[tok_at(k, 0)])
        along_z(k + 1, held(tok_at(-k, 0)), held(tok_at(k, 0)))
        along_x(-k, held(tok_at(-k, 0)))
        along_x(k, held(tok_at(k, 0)))
        if k == 1:
            next_at = ((x + 1) % X) // 2 + y * 2
            arrived(("relay", "win"), relay_in)
            start(("relay2", "win"), relay_in, win_own.at[next_at], x_down)
            arrived(("relay", "wout"), relay_out)
            start(("relay2", "wout"), relay_out, wout_own.at[next_at], x_down)
            from_x(0)
            from_y(0)
        if k == 2:
            from_x(-1)
            from_x(1)
            from_y_far(0)
        if k == 3:
            across_at = grp_at(0, 1)
            arrived(("relay2", "win"), win_own.at[across_at])
            arrived(("relay2", "wout"), wout_own.at[across_at])
            along_y(1, expert_held(across_at))
            from_x(-2)
            from_x(2)

    at = tok_at(4, 0)
    arrived(("up", "pre", 4), pre_all.at[at])
    arrived(("up", "qkv", 4), qkv_all.at[at])
    arrived(("down", "wo", 4), wo_all.at[at])
    along_x(4, held(at))
    from_x(-3)
    from_x(3)
    from_y(1)
    from_x(4)
    from_y_far(1)

    for dz in (0, -1, 1, -2, 2, -3, 3, 4):
        for parity in (0, 1):
            at = tok_at(dz, parity, 1)
            for name, ref in (("pre", pre_all), ("qkv", qkv_all), ("wo", wo_all)):
                arrived(("mate", name, dz, parity), ref.at[at])
    for dy in (0, -1, 1, 2):
        for across in (0, 1):
            at = grp_at(dy, across)
            arrived(("mate", "win", dy, across), win_other.at[at])
            arrived(("mate", "wout", dy, across), wout_other.at[at])
    for copy in own:
        copy.wait()
    for copy in sends:
        copy.wait_send()


def gather_all(qkv, wo, pre, win, wout):
    dtype = jnp.bfloat16
    tok, grp = lax.axis_size("tok"), lax.axis_size("grp")
    shapes = [(tok,) + a.shape for a in (qkv, wo, pre)]
    shapes += [(grp,) + win.shape] * 2 + [(grp,) + wout.shape] * 2
    return pl.pallas_call(
        gather_kernel,
        out_shape=[jax.ShapeDtypeStruct(shape, dtype) for shape in shapes],
        in_specs=[pl.BlockSpec(memory_space=pltpu.VMEM)] * 5,
        out_specs=[pl.BlockSpec(memory_space=pl.ANY)] * 7,
        scratch_shapes=[
            pltpu.VMEM(win.shape, dtype),
            pltpu.VMEM(wout.shape, dtype),
            pltpu.SemaphoreType.DMA((N_COPIES,)),
            pltpu.SemaphoreType.DMA((N_COPIES,)),
            pltpu.SemaphoreType.DMA((5,)),
        ],
        compiler_params=pltpu.CompilerParams(collective_id=0, has_side_effects=True),
    )(qkv, wo, pre, win, wout)


def exchange_kernel(rows, got, send, recv, local):
    g, t = lax.axis_index("grp"), lax.axis_index("tok")
    chip, core = t // 2, t % 2
    chips = rows.shape[0]
    others = [(chip + step) % chips for step in range(1, chips)]
    greet([(g, other * 2 + core) for other in others])
    keep = pltpu.make_async_copy(rows.at[chip], got.at[chip], local)
    keep.start()
    copies = []
    for n, other in enumerate(others):
        copy = pltpu.make_async_remote_copy(
            src_ref=rows.at[other], dst_ref=got.at[chip], send_sem=send.at[n],
            recv_sem=recv.at[n], device_id=(g, other * 2 + core), device_id_type=MESH,
        )
        copy.start()
        copies.append(copy)
    for n in range(chips - 1):
        source = (chip + chips - 1 - n) % chips
        pltpu.make_async_remote_copy(
            src_ref=got.at[source], dst_ref=got.at[source], send_sem=send.at[n],
            recv_sem=recv.at[n], device_id=(g, others[n] * 2 + core), device_id_type=MESH,
        ).wait_recv()
    for copy in copies:
        copy.wait_send()
    keep.wait()


def exchange(rows, collective_id):
    count = rows.shape[0] - 1
    return pl.pallas_call(
        exchange_kernel,
        out_shape=jax.ShapeDtypeStruct(rows.shape, rows.dtype),
        in_specs=[pl.BlockSpec(memory_space=pltpu.VMEM)],
        out_specs=pl.BlockSpec(memory_space=pltpu.VMEM),
        scratch_shapes=[
            pltpu.SemaphoreType.DMA((count,)),
            pltpu.SemaphoreType.DMA((count,)),
            pltpu.SemaphoreType.DMA,
        ],
        compiler_params=pltpu.CompilerParams(
            collective_id=collective_id, has_side_effects=True
        ),
    )(rows)


def attend(soft_state, queries, key_block, allowed):
    maxima, totals, numerators = soft_state
    kv_width = key_block.shape[1] // 2
    key_rows = key_block[:, :kv_width].reshape(
        key_block.shape[0], queries.shape[1], queries.shape[3]
    )
    value_rows = key_block[:, kv_width:].reshape(
        key_block.shape[0], queries.shape[1], queries.shape[3]
    )
    scores = jnp.einsum(
        "tkgd,skd->tkgs", queries, key_rows, preferred_element_type=jnp.float32
    ) * queries.shape[3] ** (-0.5)
    if allowed is not None:
        scores = jnp.where(allowed[:, None, None, :], scores, -jnp.inf)
    new_max = jnp.maximum(maxima, jnp.max(scores, axis=-1))
    rescale = jnp.exp(maxima - new_max)
    weights = jnp.exp(scores - new_max[..., None])
    totals = totals * rescale + jnp.sum(weights, axis=-1)
    numerators = numerators * rescale[..., None] + jnp.einsum(
        "tkgs,skd->tkgd",
        weights.astype(jnp.bfloat16),
        value_rows,
        preferred_element_type=jnp.float32,
    )
    return (new_max, totals, numerators)


def on_device(
    layer_input,
    attn_gain,
    w_query,
    w_keyval,
    w_output,
    prefix_cache,
    lengths,
    moe_gain,
    w_router,
    routes,
    w_expert_in,
    w_expert_out,
):
    tokens = layer_input[0]
    row_count = tokens.shape[0]
    model_width = tokens.shape[1]
    group_share = HEADS // KV_HEADS
    normed = rms_scale(tokens, attn_gain).astype(jnp.bfloat16)
    qkv_all, wo_all, pre_all, win_own, win_other, wout_own, wout_other = gather_all(
        jnp.concatenate([w_query, w_keyval], axis=1),
        w_output,
        prefix_cache[0],
        w_expert_in[0],
        w_expert_out[0],
    )
    projected = product(normed, qkv_all.reshape(model_width, -1)).astype(jnp.bfloat16)
    queries = projected[:, :model_width].reshape(row_count, KV_HEADS, group_share, HEAD_DIM)
    keyval = projected[:, model_width:]
    position = lax.axis_index("tok")
    positions = position * row_count + jnp.arange(row_count, dtype=jnp.int32)
    req_lengths = lengths[0]
    own_seg = segment_of(req_lengths, positions)
    before_seg = jnp.where(
        positions >= row_count, segment_of(req_lengths, positions - row_count), -1
    )
    earlier = passed_along(keyval, "tok", 1)
    near_block = jnp.concatenate([earlier, keyval], axis=0)
    near_seg = jnp.concatenate([before_seg, own_seg])
    near_pos = jnp.concatenate([positions - row_count, positions])
    allowed = (near_seg[None, :] == own_seg[:, None]) & (near_pos[None, :] <= positions[:, None])
    soft_state = (
        jnp.full((row_count, KV_HEADS, group_share), -jnp.inf, jnp.float32),
        jnp.zeros((row_count, KV_HEADS, group_share), jnp.float32),
        jnp.zeros((row_count, KV_HEADS, group_share, HEAD_DIM), jnp.float32),
    )
    soft_state = attend(soft_state, queries, near_block, allowed)
    prefix_whole = pre_all.reshape(-1, pre_all.shape[2])
    maxima, totals, numerators = attend(soft_state, queries, prefix_whole, None)
    attended = (
        (numerators / totals[..., None]).astype(jnp.bfloat16).reshape(row_count, HEADS * HEAD_DIM)
    )
    columns = attended
    residual = tokens.astype(jnp.float32) + product(
        columns, wo_all.reshape(-1, model_width)
    )
    normed2 = rms_scale(residual, moe_gain).astype(jnp.bfloat16)
    logits = product(normed2, w_router)
    experts = w_router.shape[1]
    chosen = routes[0]
    expert_marks = chosen[:, :, None] == jnp.arange(experts, dtype=jnp.int32)
    picked = jnp.sum(jnp.where(expert_marks, logits[:, None, :], 0.0), axis=-1)
    scores = jax.nn.sigmoid(picked)
    gate_weights = scores / jnp.sum(scores, axis=-1, keepdims=True)
    flat_routes = chosen.reshape(-1)
    flat_marks = expert_marks.reshape(-1, experts).astype(jnp.int32)
    prior_count = jnp.cumsum(flat_marks, axis=0, dtype=jnp.int32) - flat_marks
    slot_index = jnp.sum(prior_count * flat_marks, axis=1)
    target = (flat_routes * SLOTS + slot_index).reshape(row_count, TOP)
    slot_ids = jnp.arange(experts * SLOTS, dtype=jnp.int32)
    first, second = target[:, 0], target[:, 1]
    place = (first[None, :] == slot_ids[:, None]) | (second[None, :] == slot_ids[:, None])
    outgoing = product(place.astype(jnp.bfloat16), normed2).astype(jnp.bfloat16)
    arrived = exchange(outgoing.reshape(experts, SLOTS, model_width), 1)
    flat_rows = arrived.reshape(-1, model_width)

    def half_expert(w_in, w_out):
        gate_up = product(flat_rows, w_in.reshape(model_width, -1))
        half_units = gate_up.shape[1] // 2
        act = (jax.nn.silu(gate_up[:, :half_units]) * gate_up[:, half_units:]).astype(jnp.bfloat16)
        return product(act, w_out.reshape(half_units, model_width))

    expert_out = half_expert(win_own, wout_own) + half_expert(win_other, wout_other)
    returned = exchange(
        expert_out.astype(jnp.bfloat16).reshape(experts, SLOTS, model_width), 2
    )
    results = returned.reshape(-1, model_width)
    gates = jnp.where(first[:, None] == slot_ids[None, :], gate_weights[:, :1], 0.0)
    gates += jnp.where(second[:, None] == slot_ids[None, :], gate_weights[:, 1:], 0.0)
    gates_high = lax.reduce_precision(gates, exponent_bits=8, mantissa_bits=7)
    gates_low = (gates - gates_high).astype(jnp.bfloat16)
    weighted = product(gates_high.astype(jnp.bfloat16), results) + product(gates_low, results)
    hidden = (residual + weighted).astype(jnp.bfloat16)
    return (hidden[None], keyval[None])


def solution(mesh):
    in_specs = (
        P("grp", "tok", None),
        P(),
        P("tok", None),
        P("tok", None),
        P("tok", None),
        P("grp", "tok", None),
        P("grp", None),
        P(),
        P(),
        P("grp", "tok", None),
        P("tok", "grp", None),
        P("tok", "grp", None),
    )
    out_specs = (P("grp", "tok", None), P("grp", "tok", None))
    return jax.shard_map(
        on_device, mesh=mesh, in_specs=in_specs, out_specs=out_specs, check_vma=False
    )
```
